256 devices in a mesh: query: 16 (over z, y_lo), db: 16 (over x, y_hi, core).
Axes of the slice: x: 4, y: 4 (y_hi: 2, y_lo: 2; y = y_hi * 2 + y_lo), z: 8, core: 2. Of those that a mesh axis runs over, the one named last changes fastest.
Arguments:
- noisy_images: float32 [16, 3, 128, 128], P('db', None, 'query'), may hold values from -6 to 6
- database: bfloat16 [432, 262144], P(None, 'db'), may hold values from -4 to 4
- picked_blocks: int32 [16, 4], P('db'), may hold values from 0 to 7, as said below
- alpha_now: float32 [16], replicated, may hold values from 0.15 to 0.35
- alpha_next: float32 [16], replicated, may hold values from 0.4 to 0.8
Outputs:
- next_images: float32 [16, 3, 128, 128], P('db', None, 'query')
The draws below stay inside these ranges and needn't reach their ends.
Inputs may be any that keep to these rules, and one draw needn't show every extreme that they name: `picked_blocks`: each row names 4 different windows of the 8 stored on that shard.
All inputs are finite; a program needn't handle non-finite values.
Results may differ from the reference program's by a relative error of at most 0.00075.
Values may be sent and summed in bfloat16 or wider, within the bound.
A program may use at most 192 MiB of HBM per device.

```python
import math
from functools import partial
import jax
import jax.numpy as jnp
from jax import lax

W = 128
BLOCK = 2048
BLOCKS_DEV = 8
WINDOWS = 4
SHARDS = 16
IMAGES = 16
HEIGHT = 128
DB_COLS = 262144


def pick_row(row_key):
    return jax.random.permutation(row_key, BLOCKS_DEV)[:WINDOWS]


def lattice_mask():
    entry_index = jnp.arange(432)
    channel = entry_index // 144
    within = entry_index % 144
    on_grid = (channel == 0) & (within // 12 % 4 == 0) & (within % 12 % 4 == 0)
    return jnp.where(on_grid, 1.0, 0.0).astype(jnp.float32)


def signal_draw(key):
    spread = jnp.exp(jax.random.uniform(jax.random.fold_in(key, 21), (IMAGES,), jnp.float32, jnp.log(0.15), jnp.log(0.35)))
    hushed = jax.random.uniform(jax.random.fold_in(key, 22), (IMAGES,), jnp.float32, 0.33, 0.35)
    ladder = jax.random.uniform(jax.random.fold_in(key, 23), (IMAGES,), jnp.float32, 0.15, 0.17)
    image_kind = jnp.arange(IMAGES) % 4
    chosen = jnp.where(image_kind == 1, hushed, jnp.where(image_kind == 3, ladder, spread))
    return jnp.clip(chosen, 0.15, 0.35)


def shared_draw(key):
    pick_keys = jax.random.split(jax.random.fold_in(key, 11), SHARDS)
    chosen = jax.vmap(pick_row)(pick_keys).astype(jnp.int32)
    odd_shard = jax.random.randint(jax.random.fold_in(key, 17), (), 0, SHARDS)
    scales = jnp.exp(jax.random.uniform(jax.random.fold_in(key, 18), (1, DB_COLS), jnp.float32, jnp.log(0.5), jnp.log(2.0)))
    entries = jax.random.normal(jax.random.fold_in(key, 12), (432, DB_COLS), jnp.float32) * scales
    shard_of = jnp.arange(DB_COLS) // (BLOCKS_DEV * BLOCK)
    offsets = jnp.where(shard_of == odd_shard, -1.5, 1.5).astype(jnp.float32)
    entries = entries + lattice_mask()[:, None] * offsets[None, :]
    return (chosen, jnp.clip(entries, -4.0, 4.0))


def draw_database(key, part):
    return shared_draw(key)[1].astype(jnp.bfloat16)


def draw_picked_blocks(key, part):
    return shared_draw(key)[0]


def draw_alpha_now(key, part):
    return signal_draw(key)


def draw_noisy_images(key, part):
    signal = signal_draw(key)
    image_kind = jnp.arange(IMAGES) % 4
    loudness = jnp.where(image_kind == 1, 0.05, jnp.where(image_kind == 3, 0.15, 1.0)).astype(jnp.float32)
    images = 0.7 * jax.random.normal(jax.random.fold_in(key, 13), (IMAGES, 3, HEIGHT, W), jnp.float32)
    images = jnp.clip(images, -4.0, 4.0) * loudness[:, None, None, None]
    linear = jnp.sqrt(signal) / (1.0 - signal)
    row_index = jnp.arange(HEIGHT)
    col_index = jnp.arange(W)
    levels = jnp.array([7.3, 7.6, 7.9, 8.3, 7.1, 7.45, 7.75, 8.1], jnp.float32)
    level_index = (row_index[None, :, None] // 32 + 3 * (col_index[None, None, :] // 32) + jnp.arange(IMAGES)[:, None, None]) % 8
    target = -levels[level_index] / (27.0 * linear[:, None, None])
    target = target + 0.02 * jax.random.normal(jax.random.fold_in(key, 24), (IMAGES, HEIGHT, W), jnp.float32)
    on_grid = ((row_index % 4 == 0)[:, None] & (col_index % 4 == 0)[None, :])[None, :, :] & (image_kind == 3)[:, None, None]
    images = images.at[:, 0].set(jnp.where(on_grid, target, images[:, 0]))
    return jnp.clip(images, -6.0, 6.0)


def setup_inputs(seed: int = 0) -> dict:
    streams_of = jax.random.split(jax.random.key(seed), 6)
    return {
        "noisy_images": draw_noisy_images(jax.random.fold_in(streams_of[5], 71), 0),
        "database": draw_database(jax.random.fold_in(streams_of[5], 71), 0),
        "picked_blocks": draw_picked_blocks(jax.random.fold_in(streams_of[5], 71), 0),
        "alpha_now": draw_alpha_now(jax.random.fold_in(streams_of[5], 71), 0),
        "alpha_next": jnp.clip(jnp.exp(jax.random.uniform(streams_of[4], (IMAGES,), jnp.float32, math.log(0.4), math.log(0.8))), 0.4, 0.8),
    }


def extract(images):
    slab_list = []
    for row_shift in range(12):
        for col_shift in range(12):
            rolled = jnp.roll(images, (-row_shift, -col_shift), axis=(2, 3))
            slab_list.append(rolled[:, :, ::4, ::4])
    stacked = jnp.stack(slab_list)
    stacked = stacked.reshape(12, 12, stacked.shape[1], 3, stacked.shape[3], stacked.shape[4])
    stacked = jnp.transpose(stacked, (3, 0, 1, 2, 4, 5))
    return stacked.reshape(432, stacked.shape[3], -1).astype(jnp.bfloat16)

def posterior(database, picked_blocks, pair):
    patch_cols, signal = pair
    linear = jnp.sqrt(signal) / (1.0 - signal)
    quadratic = signal / (2.0 * (1.0 - signal))
    count = patch_cols.shape[1]

    def visit(carry, number):
        maxima, totals, numerator = carry
        shard = number // WINDOWS
        slot = number % WINDOWS
        offset = ((shard * BLOCKS_DEV + picked_blocks[shard, slot]) * BLOCK).astype(jnp.int32)
        window = lax.dynamic_slice_in_dim(database, offset, BLOCK, 1)
        squares = lax.optimization_barrier(jnp.sum(window.astype(jnp.float32) ** 2, axis=0))
        inner = jnp.dot(patch_cols.T, window, preferred_element_type=jnp.float32)
        logits = linear * inner - quadratic * squares[None, :]
        new_max = jnp.maximum(maxima, lax.optimization_barrier(jnp.max(logits, axis=1)))
        rescale = jnp.exp(maxima - new_max)
        raw = jnp.exp(logits - new_max[:, None])
        totals = totals * rescale + lax.optimization_barrier(jnp.sum(raw, axis=1))
        numerator = numerator * rescale[None, :] + jnp.dot(window, raw.astype(jnp.bfloat16).T, preferred_element_type=jnp.float32)
        return ((new_max, totals, numerator), None)
    start = (jnp.full((count,), -jnp.inf, jnp.float32), jnp.zeros((count,), jnp.float32), jnp.zeros((432, count), jnp.float32))
    final, _ = lax.scan(visit, start, jnp.arange(SHARDS * WINDOWS, dtype=jnp.int32))
    return final[2] / final[1][None, :]

def reference(noisy_images, database, picked_blocks, alpha_now, alpha_next):
    patches = extract(noisy_images)
    estimates = lax.map(partial(posterior, database, picked_blocks), (jnp.transpose(patches, (1, 0, 2)), alpha_now))
    count_images, channels, height, across = noisy_images.shape
    estimates = estimates.reshape(count_images, 3, 12, 12, height // 4, across // 4)
    denoised = jnp.zeros(noisy_images.shape, jnp.float32)
    for row_shift in range(12):
        for col_shift in range(12):
            placed = jnp.zeros(noisy_images.shape, jnp.float32).at[:, :, ::4, ::4].set(estimates[:, :, row_shift, col_shift])
            denoised = denoised + jnp.roll(placed, (row_shift, col_shift), axis=(2, 3))
    denoised = denoised / 9.0
    signal = alpha_now[:, None, None, None]
    after = alpha_next[:, None, None, None]
    noise_part = (noisy_images - jnp.sqrt(signal) * denoised) / jnp.sqrt(1.0 - signal)
    return jnp.sqrt(after) * denoised + jnp.sqrt(1.0 - after) * noise_part
```

```python
import functools

import jax
import jax.numpy as jnp
from jax import lax
from jax.experimental import pallas as pl
from jax.experimental.pallas import tpu as pltpu
from jax.sharding import PartitionSpec as P

MESH = pl.DeviceIdType.MESH
F32 = jnp.float32
BF16 = jnp.bfloat16
BLOCK = 2048
PREP = 512
STEP = 512
LOG2E = 1.4426950408889634


def step_kernel(nq, nd, noisy_ref, db_hbm, picked_ref, now_ref, next_ref, out_ref,
                dbv, kt, sbuf0, sbuf1, qbuf, acc, sel, perm, ystack, zbuf, gath, stat, pstage, precv,
                dbsem, gss, grs, sts, srs, pss, prs):
    ng = nd // 4
    keys = kt.shape[0]
    q = lax.axis_index("query")
    d = lax.axis_index("db")
    up = lax.rem(q + nq - 1, nq)
    down = lax.rem(q + 1, nq)
    lo_me = d // ng
    g_me = lax.rem(d, ng)

    def db_copy(i):
        return pltpu.make_async_copy(db_hbm.at[:, pl.ds(i * BLOCK, BLOCK)], dbv.at[i], dbsem.at[i])

    for i in range(dbv.shape[0]):
        db_copy(i).start()

    barrier = pltpu.get_barrier_semaphore()

    def greet(row, first):
        def body(o, carry):
            pl.semaphore_signal(barrier, inc=1, device_id=(row, lax.rem(d + o, nd)), device_id_type=MESH)
            return carry
        lax.fori_loop(first, nd, body, 0)

    greet(q, 1)
    greet(up, 0)
    greet(down, 0)

    own_tile = noisy_ref[0].astype(BF16)
    gath[0, lo_me, g_me] = own_tile

    def fill_sel(j, carry):
        lane = lax.broadcasted_iota(jnp.int32, (512, 128), 1)
        row = lax.broadcasted_iota(jnp.int32, (512, 128), 0)
        want = (lane // 32) * 128 + (4 * (lane % 32) + j) % 128
        sel[:, pl.ds(pl.multiple_of(j * 128, 128), 128)] = jnp.where(row == want, 1.0, 0.0).astype(BF16)
        return carry

    lax.fori_loop(0, 12, fill_sel, 0)

    def fill_perm(r, carry):
        row = lax.broadcasted_iota(jnp.int32, (144, 192), 0)
        col = lax.broadcasted_iota(jnp.int32, (144, 192), 1)
        want = (row % 12) * 16 + 4 * r + row // 12
        perm[pl.ds(pl.multiple_of(r * 144, 144), 144), :] = jnp.where(col == want, 1.0, 0.0).astype(BF16)
        return carry

    lax.fori_loop(0, 2, fill_perm, 0)

    pl.semaphore_wait(barrier, 3 * nd - 1)

    def tile_same(src):
        lo, g = src // ng, lax.rem(src, ng)
        return gath.at[0, lo, g]

    def send_same(o, carry):
        pltpu.make_async_remote_copy(
            src_ref=gath.at[0, lo_me, g_me], dst_ref=gath.at[0, lo_me, g_me],
            send_sem=gss.at[o], recv_sem=grs.at[d],
            device_id=(q, lax.rem(d + o, nd)), device_id_type=MESH).start()
        return carry

    def send_up(o, carry):
        pltpu.make_async_remote_copy(
            src_ref=gath.at[0, lo_me, g_me], dst_ref=gath.at[1, lo_me, g_me],
            send_sem=gss.at[nd + o], recv_sem=grs.at[nd + d],
            device_id=(up, lax.rem(d + o, nd)), device_id_type=MESH).start()
        return carry

    lax.fori_loop(1, nd, send_same, 0)
    lax.fori_loop(0, nd, send_up, 0)

    for i in range(dbv.shape[0]):
        db_copy(i).wait()

    def key_columns(i, size):
        slot = i // (BLOCK // size)
        inside = pl.multiple_of(lax.rem(i, BLOCK // size) * size, size)
        return dbv[picked_ref[0, slot], :, pl.ds(inside, size)]

    def prepare(i, carry):
        cols = key_columns(i, PREP)
        wide = cols.astype(F32)
        squares = jnp.sum(wide * wide, axis=0, keepdims=True)
        high = squares.astype(BF16).astype(F32)
        rest = squares - high
        mid = rest.astype(BF16).astype(F32)
        low = rest - mid
        row = lax.broadcasted_iota(jnp.int32, (80, PREP), 0)
        extra = jnp.where((row == 0) | (row == 3) | (row == 5), high,
                          jnp.where((row == 1) | (row == 4), mid, jnp.where(row == 2, low, 0.0)))
        full = jnp.concatenate([cols, extra.astype(BF16)], axis=0)
        kt[pl.ds(pl.multiple_of(i * PREP, PREP), PREP), :] = full.T
        return carry

    lax.fori_loop(0, keys // PREP, prepare, 0)

    def per_lane(ref, g, rows):
        lane = lax.broadcasted_iota(jnp.int32, (rows, 256), 1)
        image = (lane // 32) % 4
        value = jnp.full((rows, 256), ref[g], F32)
        for lo in range(1, 4):
            value = jnp.where(image == lo, ref[lo * ng + g], value)
        return value

    for g in range(ng):
        a = per_lane(now_ref, g, 80)
        c = -0.5 * jnp.sqrt(a)
        high = c.astype(BF16).astype(F32)
        rest = c - high
        mid = rest.astype(BF16).astype(F32)
        low = rest - mid
        row = lax.broadcasted_iota(jnp.int32, (80, 256), 0)
        extra = jnp.where(row < 3, high, jnp.where(row < 5, mid, jnp.where(row == 5, low, 0.0)))
        qbuf[g, pl.ds(432, 80), :] = extra.astype(BF16)

    def got_same(o, carry):
        src = lax.rem(d + o, nd)
        lo, g = src // ng, lax.rem(src, ng)
        pltpu.make_async_remote_copy(
            src_ref=gath.at[0, lo, g], dst_ref=gath.at[0, lo, g], send_sem=gss.at[o], recv_sem=grs.at[src],
            device_id=(q, src), device_id_type=MESH).wait_recv()
        return carry

    def got_below(o, carry):
        src = lax.rem(d + o, nd)
        lo, g = src // ng, lax.rem(src, ng)
        pltpu.make_async_remote_copy(
            src_ref=gath.at[1, lo, g], dst_ref=gath.at[1, lo, g], send_sem=gss.at[nd + o], recv_sem=grs.at[nd + src],
            device_id=(down, src), device_id_type=MESH).wait_recv()
        return carry

    lax.fori_loop(1, nd, got_same, 0)
    lax.fori_loop(0, nd, got_below, 0)

    lanes = []
    for lo in range(4):
        both = jnp.concatenate([gath[0, lo].astype(F32), gath[1, lo].astype(F32)], axis=2)
        lanes.append(both.reshape(ng * 48, 128))
    rows = jnp.concatenate(lanes, axis=1).astype(BF16)
    for j in range(12):
        y = jnp.dot(rows, sel[:, j * 128:(j + 1) * 128], preferred_element_type=F32).astype(BF16)
        for g in range(ng):
            for c in range(3):
                ystack[c, j * 16:(j + 1) * 16, g * 128:(g + 1) * 128] = y[(g * 3 + c) * 16:(g * 3 + c + 1) * 16, :]
    for c in range(3):
        placed = jnp.dot(perm[...], ystack[c], preferred_element_type=F32).astype(BF16)
        for g in range(ng):
            for r in range(2):
                qbuf[g, c * 144:(c + 1) * 144, r * 128:(r + 1) * 128] = (
                    placed[r * 144:(r + 1) * 144, g * 128:(g + 1) * 128])

    sbufs = (sbuf0, sbuf1)
    steps = keys // STEP

    def logits(g, i):
        part = pl.ds(pl.multiple_of(i * STEP, STEP), STEP)
        s = jnp.dot(kt[part, :], qbuf[g], preferred_element_type=F32)
        sbufs[g % 2][part, :] = s
        return jnp.max(s.reshape(STEP // 8, 8, 256), axis=0)

    def weigh(g, i, top, scale):
        part = pl.ds(pl.multiple_of(i * STEP, STEP), STEP)
        p = jnp.exp2((sbufs[g % 2][part, :] - top) * scale)
        cols = key_columns(i, STEP)
        acc[g] += jnp.dot(cols, p.astype(BF16), preferred_element_type=F32)
        return jnp.sum(p.reshape(STEP // 8, 8, 256), axis=0)

    def scale_of(g):
        a = per_lane(now_ref, g, 1)
        return LOG2E * jnp.sqrt(a) / (1.0 - a)

    def stat_send(g, o):
        return pltpu.make_async_remote_copy(
            src_ref=stat.at[g, d], dst_ref=stat.at[g, d], send_sem=sts.at[g, o], recv_sem=srs.at[g, d],
            device_id=(q, lax.rem(d + o, nd)), device_id_type=MESH)

    def share(g, top, total):
        whole = jnp.concatenate([top[:, :128], top[:, 128:], total[:, :128], total[:, 128:],
                                 jnp.zeros((4, 128), F32)], axis=0)
        stat[g, d] = whole

        def body(o, carry):
            stat_send(g, o).start()
            return carry

        lax.fori_loop(1, nd, body, 0)

    def pixel_send(g, lo, half):
        dest = lo * ng + g
        return pltpu.make_async_remote_copy(
            src_ref=pstage.at[g, lo, half], dst_ref=precv.at[half, d],
            send_sem=pss.at[g, 2 * lo + half], recv_sem=prs.at[half, d],
            device_id=(down if half else q, dest), device_id_type=MESH)

    def finish(g, top, scale):
        def body(o, carry):
            src = lax.rem(d + o, nd)
            pltpu.make_async_remote_copy(
                src_ref=stat.at[g, src], dst_ref=stat.at[g, src], send_sem=sts.at[g, o], recv_sem=srs.at[g, src],
                device_id=(q, src), device_id_type=MESH).wait_recv()
            return carry

        lax.fori_loop(1, nd, body, 0)
        every = stat[g]
        tops = jnp.concatenate([every[:, 0], every[:, 1]], axis=1)
        totals = jnp.concatenate([every[:, 2], every[:, 3]], axis=1)
        highest = jnp.max(tops, axis=0, keepdims=True)
        total = jnp.sum(totals * jnp.exp2((tops - highest) * scale), axis=0, keepdims=True)
        factor = jnp.exp2((top - highest) * scale) / (9.0 * total)
        num = acc[g] * factor
        for c in range(3):
            first = num[c * 144:(c + 1) * 144, :128]
            second = num[c * 144:(c + 1) * 144, 128:]
            zbuf[c * 192:c * 192 + 48, :] = first[:48]
            zbuf[c * 192 + 48:c * 192 + 144, :] = first[48:] + second[:96]
            zbuf[c * 192 + 144:c * 192 + 192, :] = second[96:]
        parts = []
        for j in range(12):
            parts.append(zbuf[pl.ds(j, 48, stride=12), :])
        flat = jnp.concatenate(parts, axis=1)
        high = flat.astype(BF16)
        low = (flat - high.astype(F32)).astype(BF16)
        both = jnp.concatenate([high, low], axis=0)
        pix = lax.dot_general(both, sel[...], (((1,), (1,)), ((), ())), preferred_element_type=F32)
        pix = pix[:48] + pix[48:]
        for lo in range(4):
            tile = pix[:, lo * 128:(lo + 1) * 128].reshape(3, 16, 128)
            pstage[g, lo, 0] = tile[:, :8]
            pstage[g, lo, 1] = tile[:, 8:]
        for lo in range(4):
            @pl.when(lo * ng + g != d)
            def _():
                pixel_send(g, lo, 0).start()
            pixel_send(g, lo, 1).start()

    neg = jnp.full((8, 256), -jnp.inf, F32)
    tops = {}
    scales = {}
    for t in range(ng + 1):
        if t >= 1:
            scales[t - 1] = scale_of(t - 1)
            acc[t - 1] = jnp.zeros((432, 256), F32)

        def body(i, carry, t=t):
            best, total = carry
            if t < ng:
                best = jnp.maximum(best, logits(t, i))
            if t >= 1:
                total = total + weigh(t - 1, i, tops[t - 1], scales[t - 1])
            return best, total

        best, total = lax.fori_loop(0, steps, body, (neg, jnp.zeros((8, 256), F32)))
        if t < ng:
            tops[t] = jnp.max(best, axis=0, keepdims=True)
        if t >= 1:
            share(t - 1, tops[t - 1], jnp.sum(total, axis=0, keepdims=True))
        if t >= 2:
            finish(t - 2, tops[t - 2], scales[t - 2])
    finish(ng - 1, tops[ng - 1], scales[ng - 1])

    def got_own(o, carry):
        src = lax.rem(d + o, nd)
        pltpu.make_async_remote_copy(
            src_ref=precv.at[0, src], dst_ref=precv.at[0, src], send_sem=pss.at[0, 0], recv_sem=prs.at[0, src],
            device_id=(q, src), device_id_type=MESH).wait_recv()
        return carry

    def got_spill(o, carry):
        src = lax.rem(d + o, nd)
        pltpu.make_async_remote_copy(
            src_ref=precv.at[1, src], dst_ref=precv.at[1, src], send_sem=pss.at[0, 1], recv_sem=prs.at[1, src],
            device_id=(up, src), device_id_type=MESH).wait_recv()
        return carry

    lax.fori_loop(1, nd, got_own, 0)
    lax.fori_loop(0, nd, got_spill, 0)
    precv[0, d] = pstage[g_me, lo_me, 0]
    denoised = jnp.sum(precv[0], axis=0) + jnp.sum(precv[1], axis=0)
    signal = jnp.full((1, 8, 128), now_ref[d], F32)
    after = jnp.full((1, 8, 128), next_ref[d], F32)
    noise = (noisy_ref[0] - jnp.sqrt(signal) * denoised) / jnp.sqrt(1.0 - signal)
    out_ref[0] = jnp.sqrt(after) * denoised + jnp.sqrt(1.0 - after) * noise

    def sent_same(o, carry):
        pltpu.make_async_remote_copy(
            src_ref=gath.at[0, lo_me, g_me], dst_ref=gath.at[0, lo_me, g_me],
            send_sem=gss.at[o], recv_sem=grs.at[d],
            device_id=(q, lax.rem(d + o, nd)), device_id_type=MESH).wait_send()
        return carry

    def sent_up(o, carry):
        pltpu.make_async_remote_copy(
            src_ref=gath.at[0, lo_me, g_me], dst_ref=gath.at[1, lo_me, g_me],
            send_sem=gss.at[nd + o], recv_sem=grs.at[nd + d],
            device_id=(up, lax.rem(d + o, nd)), device_id_type=MESH).wait_send()
        return carry

    lax.fori_loop(1, nd, sent_same, 0)
    lax.fori_loop(0, nd, sent_up, 0)
    for g in range(ng):
        def sent_stat(o, carry, g=g):
            stat_send(g, o).wait_send()
            return carry

        lax.fori_loop(1, nd, sent_stat, 0)
        for lo in range(4):
            @pl.when(lo * ng + g != d)
            def _():
                pixel_send(g, lo, 0).wait_send()
            pixel_send(g, lo, 1).wait_send()


def on_device(nq, nd, noisy, database, picked, now, after):
    ng = nd // 4
    windows = picked.shape[1]
    keys = windows * BLOCK
    vmem = pl.BlockSpec(memory_space=pltpu.VMEM)
    smem = pl.BlockSpec(memory_space=pltpu.SMEM)
    dma = pltpu.SemaphoreType.DMA
    return pl.pallas_call(
        functools.partial(step_kernel, nq, nd),
        out_shape=jax.ShapeDtypeStruct(noisy.shape, F32),
        in_specs=[vmem, pl.BlockSpec(memory_space=pl.ANY), smem, smem, smem],
        out_specs=vmem,
        scratch_shapes=[
            pltpu.VMEM((database.shape[1] // BLOCK, database.shape[0], BLOCK), BF16),
            pltpu.VMEM((keys, 512), BF16),
            pltpu.VMEM((keys, 256), F32),
            pltpu.VMEM((keys, 256), F32),
            pltpu.VMEM((ng, 512, 256), BF16),
            pltpu.VMEM((ng, 432, 256), F32),
            pltpu.VMEM((512, 1536), BF16),
            pltpu.VMEM((288, 192), BF16),
            pltpu.VMEM((3, 192, ng * 128), BF16),
            pltpu.VMEM((576, 128), F32),
            pltpu.VMEM((2, 4, ng, 3, 8, 128), BF16),
            pltpu.VMEM((ng, nd, 8, 128), F32),
            pltpu.VMEM((ng, 4, 2, 3, 8, 128), F32),
            pltpu.VMEM((2, nd, 3, 8, 128), F32),
            dma((database.shape[1] // BLOCK,)),
            dma((2 * nd,)),
            dma((2 * nd,)),
            dma((ng, nd)),
            dma((ng, nd)),
            dma((ng, 8)),
            dma((2, nd)),
        ],
        compiler_params=pltpu.CompilerParams(
            collective_id=0, has_side_effects=True, vmem_limit_bytes=64_000_000),
    )(noisy, database, picked, now, after)


def solution(mesh):
    return jax.shard_map(
        functools.partial(on_device, mesh.shape["query"], mesh.shape["db"]),
        mesh=mesh,
        in_specs=(P("db", None, "query", None), P(None, "db"), P("db", None), P(), P()),
        out_specs=P("db", None, "query", None),
        check_vma=False,
    )
```

```python
import functools

import jax
import jax.numpy as jnp
from jax import lax
from jax.experimental import pallas as pl
from jax.experimental.pallas import tpu as pltpu
from jax.sharding import PartitionSpec as P

MESH = pl.DeviceIdType.MESH
F32 = jnp.float32
BF16 = jnp.bfloat16
BLOCK = 2048
PREP = 512
STEP = 2048
SUB = 512
CHUNK = 32
LOG2E = 1.4426950408889634


def step_kernel(nq, nd, noisy_ref, db_hbm, picked_ref, now_ref, next_ref, out_ref,
                dbv, kt, sbuf0, sbuf1, wbuf0, wbuf1, qbuf, acc, sel, perm, ystack, zbuf, gath, stat, pstage, precv,
                dbsem, gss, grs, sts, srs, pss, prs):
    ng = nd // 4
    keys = kt.shape[0]
    q = lax.axis_index("query")
    d = lax.axis_index("db")
    up = lax.rem(q + nq - 1, nq)
    down = lax.rem(q + 1, nq)
    lo_me = d // ng
    g_me = lax.rem(d, ng)

    def db_copy(i):
        return pltpu.make_async_copy(db_hbm.at[:, pl.ds(i * BLOCK, BLOCK)], dbv.at[i], dbsem.at[i])

    for i in range(dbv.shape[0]):
        db_copy(i).start()

    barrier = pltpu.get_barrier_semaphore()

    def greet(row, first):
        def body(o, carry):
            pl.semaphore_signal(barrier, inc=1, device_id=(row, lax.rem(d + o, nd)), device_id_type=MESH)
            return carry
        lax.fori_loop(first, nd, body, 0)

    for row in (up, down):
        pl.semaphore_signal(barrier, inc=1, device_id=(row, d), device_id_type=MESH)
    greet(q, 1)

    own_tile = noisy_ref[0].astype(BF16)
    gath[lo_me, g_me, 0] = own_tile

    def fill_sel(j, carry):
        lane = lax.broadcasted_iota(jnp.int32, (512, 128), 1)
        row = lax.broadcasted_iota(jnp.int32, (512, 128), 0)
        want = (lane // 32) * 128 + (4 * (lane % 32) + j) % 128
        sel[:, pl.ds(pl.multiple_of(j * 128, 128), 128)] = jnp.where(row == want, 1.0, 0.0).astype(BF16)
        return carry

    lax.fori_loop(0, 12, fill_sel, 0)

    def fill_perm(r, carry):
        row = lax.broadcasted_iota(jnp.int32, (144, 192), 0)
        col = lax.broadcasted_iota(jnp.int32, (144, 192), 1)
        want = (row % 12) * 16 + 4 * r + row // 12
        perm[pl.ds(pl.multiple_of(r * 144, 144), 144), :] = jnp.where(col == want, 1.0, 0.0).astype(BF16)
        return carry

    lax.fori_loop(0, 2, fill_perm, 0)

    pl.semaphore_wait(barrier, nd + 1)

    def column_copy():
        return pltpu.make_async_remote_copy(
            src_ref=gath.at[lo_me, g_me, 0], dst_ref=gath.at[lo_me, g_me, 1],
            send_sem=gss.at[0], recv_sem=grs.at[nd + d], device_id=(up, d), device_id_type=MESH)

    def row_copy(half, o):
        return pltpu.make_async_remote_copy(
            src_ref=gath.at[lo_me, g_me, half], dst_ref=gath.at[lo_me, g_me, half],
            send_sem=gss.at[half * nd + o], recv_sem=grs.at[half * nd + d],
            device_id=(q, lax.rem(d + o, nd)), device_id_type=MESH)

    def arrival(half, src):
        lo, g = src // ng, lax.rem(src, ng)
        return pltpu.make_async_remote_copy(
            src_ref=gath.at[lo, g, half], dst_ref=gath.at[lo, g, half],
            send_sem=gss.at[half * nd + 1], recv_sem=grs.at[half * nd + src],
            device_id=(q, src), device_id_type=MESH)

    def over_peers(step):
        def body(o, carry):
            step(o)
            return carry
        lax.fori_loop(1, nd, body, 0)

    column_copy().start()
    over_peers(lambda o: row_copy(0, o).start())

    for i in range(dbv.shape[0]):
        db_copy(i).wait()

    def key_columns(i, size):
        slot = i // (BLOCK // size)
        inside = pl.multiple_of(lax.rem(i, BLOCK // size) * size, size)
        return dbv[picked_ref[0, slot], :, pl.ds(inside, size)]

    def prepare(i, carry):
        cols = key_columns(i, PREP)
        wide = cols.astype(F32)
        squares = jnp.sum(wide * wide, axis=0, keepdims=True)
        high = squares.astype(BF16).astype(F32)
        rest = squares - high
        mid = rest.astype(BF16).astype(F32)
        low = rest - mid
        row = lax.broadcasted_iota(jnp.int32, (80, PREP), 0)
        extra = jnp.where((row == 0) | (row == 3) | (row == 5), high,
                          jnp.where((row == 1) | (row == 4), mid, jnp.where(row == 2, low, 0.0)))
        full = jnp.concatenate([cols, extra.astype(BF16)], axis=0)
        kt[pl.ds(pl.multiple_of(i * PREP, PREP), PREP), :] = full.T
        return carry

    halfway = keys // PREP // 2
    lax.fori_loop(0, halfway, prepare, 0)
    column_copy().wait_recv()
    over_peers(lambda o: row_copy(1, o).start())
    lax.fori_loop(halfway, keys // PREP, prepare, 0)

    def per_lane(ref, g, rows):
        lane = lax.broadcasted_iota(jnp.int32, (rows, 256), 1)
        image = (lane // 32) % 4
        value = jnp.full((rows, 256), ref[g], F32)
        for lo in range(1, 4):
            value = jnp.where(image == lo, ref[lo * ng + g], value)
        return value

    for g in range(ng):
        a = per_lane(now_ref, g, 80)
        c = -0.5 * jnp.sqrt(a)
        high = c.astype(BF16).astype(F32)
        rest = c - high
        mid = rest.astype(BF16).astype(F32)
        low = rest - mid
        row = lax.broadcasted_iota(jnp.int32, (80, 256), 0)
        extra = jnp.where(row < 3, high, jnp.where(row < 5, mid, jnp.where(row == 5, low, 0.0)))
        qbuf[g, pl.ds(432, 80), :] = extra.astype(BF16)

    over_peers(lambda o: arrival(0, lax.rem(d + o, nd)).wait_recv())
    over_peers(lambda o: arrival(1, lax.rem(d + o, nd)).wait_recv())

    lanes = []
    for lo in range(4):
        both = jnp.concatenate([gath[lo, :, 0].astype(F32), gath[lo, :, 1].astype(F32)], axis=2)
        lanes.append(both.reshape(ng * 48, 128))
    rows = jnp.concatenate(lanes, axis=1).astype(BF16)
    for pair in range(6):
        y = jnp.dot(rows, sel[:, pair * 256:(pair + 1) * 256], preferred_element_type=F32).astype(BF16)
        for g in range(ng):
            for c in range(3):
                for k in range(2):
                    j = 2 * pair + k
                    ystack[c, j * 16:(j + 1) * 16, g * 128:(g + 1) * 128] = (
                        y[(g * 3 + c) * 16:(g * 3 + c + 1) * 16, k * 128:(k + 1) * 128])
    for c in range(3):
        placed = jnp.dot(perm[...], ystack[c], preferred_element_type=F32).astype(BF16)
        for g in range(ng):
            for r in range(2):
                qbuf[g, c * 144:(c + 1) * 144, r * 128:(r + 1) * 128] = (
                    placed[r * 144:(r + 1) * 144, g * 128:(g + 1) * 128])

    sbufs = (sbuf0, sbuf1)
    wbufs = (wbuf0, wbuf1)
    steps = keys // STEP

    def logits(g, start):
        part = pl.ds(start, SUB)
        s = jnp.dot(kt[part, :], qbuf[g], preferred_element_type=F32)
        sbufs[g % 2][part, :] = s
        return jnp.max(s.reshape(SUB // 8, 8, 256), axis=0)

    def weigh(g, start, top, scale):
        total = jnp.zeros((8, 256), F32)
        for k in range(SUB // CHUNK):
            part = pl.ds(start + k * CHUNK, CHUNK)
            p = jnp.exp2((sbufs[g % 2][part, :] - top) * scale)
            wbufs[g % 2][part, :] = p.astype(BF16)
            total = total + jnp.sum(p.reshape(CHUNK // 8, 8, 256), axis=0)
        return total

    def gather_keys(g, slot, inside, start):
        cols = dbv[picked_ref[0, slot], :, inside:inside + SUB]
        acc[g] += jnp.dot(cols, wbufs[g % 2][pl.ds(start, SUB), :], preferred_element_type=F32)

    def scale_of(g):
        a = per_lane(now_ref, g, 1)
        return LOG2E * jnp.sqrt(a) / (1.0 - a)

    def stat_send(g, o):
        return pltpu.make_async_remote_copy(
            src_ref=stat.at[g, d], dst_ref=stat.at[g, d], send_sem=sts.at[g, o], recv_sem=srs.at[g, d],
            device_id=(q, lax.rem(d + o, nd)), device_id_type=MESH)

    def share(g, top, total):
        whole = jnp.concatenate([top[:, :128], top[:, 128:], total[:, :128], total[:, 128:],
                                 jnp.zeros((4, 128), F32)], axis=0)
        stat[g, d] = whole

        def body(o, carry):
            stat_send(g, o).start()
            return carry

        lax.fori_loop(1, nd, body, 0)

    def pixel_send(g, lo, half):
        dest = lo * ng + g
        return pltpu.make_async_remote_copy(
            src_ref=pstage.at[g, lo, half], dst_ref=precv.at[half, d],
            send_sem=pss.at[g, 2 * lo + half], recv_sem=prs.at[half, d],
            device_id=(down if half else q, dest), device_id_type=MESH)

    def finish(g, top, scale):
        def body(o, carry):
            src = lax.rem(d + o, nd)
            pltpu.make_async_remote_copy(
                src_ref=stat.at[g, src], dst_ref=stat.at[g, src], send_sem=sts.at[g, o], recv_sem=srs.at[g, src],
                device_id=(q, src), device_id_type=MESH).wait_recv()
            return carry

        lax.fori_loop(1, nd, body, 0)
        every = stat[g]
        tops = jnp.concatenate([every[:, 0], every[:, 1]], axis=1)
        totals = jnp.concatenate([every[:, 2], every[:, 3]], axis=1)
        highest = jnp.max(tops, axis=0, keepdims=True)
        total = jnp.sum(totals * jnp.exp2((tops - highest) * scale), axis=0, keepdims=True)
        factor = jnp.exp2((top - highest) * scale) / (9.0 * total)
        num = acc[g] * factor
        for c in range(3):
            first = num[c * 144:(c + 1) * 144, :128]
            second = num[c * 144:(c + 1) * 144, 128:]
            zbuf[c * 192:c * 192 + 48, :] = first[:48]
            zbuf[c * 192 + 48:c * 192 + 144, :] = first[48:] + second[:96]
            zbuf[c * 192 + 144:c * 192 + 192, :] = second[96:]
        place = lax.broadcasted_iota(jnp.int32, (48, 128), 1) % 32
        parts = []
        for j in range(4):
            piece = zbuf[pl.ds(j, 48, stride=12), :]
            for k in (1, 2):
                z = zbuf[pl.ds(4 * k + j, 48, stride=12), :]
                piece = piece + jnp.where(place >= k, pltpu.roll(z, k, 1), pltpu.roll(z, 96 + k, 1))
            parts.append(piece)
        flat = jnp.concatenate(parts, axis=1)
        high = flat.astype(BF16)
        low = (flat - high.astype(F32)).astype(BF16)
        both = jnp.concatenate([high, low], axis=0)
        pix = lax.dot_general(both, sel[:, :512], (((1,), (1,)), ((), ())), preferred_element_type=F32)
        pix = pix[:48] + pix[48:]
        for lo in range(4):
            tile = pix[:, lo * 128:(lo + 1) * 128].reshape(3, 16, 128)
            pstage[g, lo, 0] = tile[:, :8]
            pstage[g, lo, 1] = tile[:, 8:]
        for lo in range(4):
            @pl.when(lo * ng + g != d)
            def _():
                pixel_send(g, lo, 0).start()
            pixel_send(g, lo, 1).start()

    neg = jnp.full((8, 256), -jnp.inf, F32)
    tops = {}
    scales = {}
    for t in range(ng + 2):
        if 1 <= t <= ng:
            scales[t - 1] = scale_of(t - 1)
        if t >= 2:
            acc[t - 2] = jnp.zeros((432, 256), F32)

        def body(i, carry, t=t):
            best, total = carry
            base = pl.multiple_of(i * STEP, STEP)
            for b in range(STEP // SUB):
                start = base + b * SUB
                if t < ng:
                    best = jnp.maximum(best, logits(t, start))
                if 1 <= t <= ng:
                    total = total + weigh(t - 1, start, tops[t - 1], scales[t - 1])
                if t >= 2:
                    gather_keys(t - 2, i, b * SUB, start)
            return best, total

        best, total = lax.fori_loop(0, steps, body, (neg, jnp.zeros((8, 256), F32)))
        if t < ng:
            tops[t] = jnp.max(best, axis=0, keepdims=True)
        if 1 <= t <= ng:
            share(t - 1, tops[t - 1], jnp.sum(total, axis=0, keepdims=True))
        if t >= 2:
            finish(t - 2, tops[t - 2], scales[t - 2])

    def got_own(o, carry):
        src = lax.rem(d + o, nd)
        pltpu.make_async_remote_copy(
            src_ref=precv.at[0, src], dst_ref=precv.at[0, src], send_sem=pss.at[0, 0], recv_sem=prs.at[0, src],
            device_id=(q, src), device_id_type=MESH).wait_recv()
        return carry

    def got_spill(o, carry):
        src = lax.rem(d + o, nd)
        pltpu.make_async_remote_copy(
            src_ref=precv.at[1, src], dst_ref=precv.at[1, src], send_sem=pss.at[0, 1], recv_sem=prs.at[1, src],
            device_id=(up, src), device_id_type=MESH).wait_recv()
        return carry

    lax.fori_loop(1, nd, got_own, 0)
    lax.fori_loop(0, nd, got_spill, 0)
    precv[0, d] = pstage[g_me, lo_me, 0]
    denoised = jnp.sum(precv[0], axis=0) + jnp.sum(precv[1], axis=0)
    signal = jnp.full((1, 8, 128), now_ref[d], F32)
    after = jnp.full((1, 8, 128), next_ref[d], F32)
    noise = (noisy_ref[0] - jnp.sqrt(signal) * denoised) / jnp.sqrt(1.0 - signal)
    out_ref[0] = jnp.sqrt(after) * denoised + jnp.sqrt(1.0 - after) * noise

    column_copy().wait_send()
    over_peers(lambda o: row_copy(0, o).wait_send())
    over_peers(lambda o: row_copy(1, o).wait_send())
    for g in range(ng):
        def sent_stat(o, carry, g=g):
            stat_send(g, o).wait_send()
            return carry

        lax.fori_loop(1, nd, sent_stat, 0)
        for lo in range(4):
            @pl.when(lo * ng + g != d)
            def _():
                pixel_send(g, lo, 0).wait_send()
            pixel_send(g, lo, 1).wait_send()


def on_device(nq, nd, noisy, database, picked, now, after):
    ng = nd // 4
    windows = picked.shape[1]
    keys = windows * BLOCK
    vmem = pl.BlockSpec(memory_space=pltpu.VMEM)
    smem = pl.BlockSpec(memory_space=pltpu.SMEM)
    dma = pltpu.SemaphoreType.DMA
    return pl.pallas_call(
        functools.partial(step_kernel, nq, nd),
        out_shape=jax.ShapeDtypeStruct(noisy.shape, F32),
        in_specs=[vmem, pl.BlockSpec(memory_space=pl.ANY), smem, smem, smem],
        out_specs=vmem,
        scratch_shapes=[
            pltpu.VMEM((database.shape[1] // BLOCK, database.shape[0], BLOCK), BF16),
            pltpu.VMEM((keys, 512), BF16),
            pltpu.VMEM((keys, 256), F32),
            pltpu.VMEM((keys, 256), F32),
            pltpu.VMEM((keys, 256), BF16),
            pltpu.VMEM((keys, 256), BF16),
            pltpu.VMEM((ng, 512, 256), BF16),
            pltpu.VMEM((ng, 432, 256), F32),
            pltpu.VMEM((512, 1536), BF16),
            pltpu.VMEM((288, 192), BF16),
            pltpu.VMEM((3, 192, ng * 128), BF16),
            pltpu.VMEM((576, 128), F32),
            pltpu.VMEM((4, ng, 2, 3, 8, 128), BF16),
            pltpu.VMEM((ng, nd, 8, 128), F32),
            pltpu.VMEM((ng, 4, 2, 3, 8, 128), F32),
            pltpu.VMEM((2, nd, 3, 8, 128), F32),
            dma((database.shape[1] // BLOCK,)),
            dma((2 * nd,)),
            dma((2 * nd,)),
            dma((ng, nd)),
            dma((ng, nd)),
            dma((ng, 8)),
            dma((2, nd)),
        ],
        compiler_params=pltpu.CompilerParams(
            collective_id=0, has_side_effects=True, vmem_limit_bytes=64_000_000),
    )(noisy, database, picked, now, after)


def solution(mesh):
    return jax.shard_map(
        functools.partial(on_device, mesh.shape["query"], mesh.shape["db"]),
        mesh=mesh,
        in_specs=(P("db", None, "query", None), P(None, "db"), P("db", None), P(), P()),
        out_specs=P("db", None, "query", None),
        check_vma=False,
    )
```

```python
import functools

import jax
import jax.numpy as jnp
from jax import lax
from jax.experimental import pallas as pl
from jax.experimental.pallas import tpu as pltpu
from jax.sharding import PartitionSpec as P

MESH = pl.DeviceIdType.MESH
F32 = jnp.float32
BF16 = jnp.bfloat16
BLOCK = 2048
PREP = 512
STEP = 2048
SUB = 512
CHUNK = 32
LOG2E = 1.4426950408889634


def step_kernel(nq, nd, noisy_ref, db_hbm, picked_ref, now_ref, next_ref, out_ref,
                dbv, kt, sbuf0, sbuf1, wbuf0, wbuf1, wbuf2, qbuf, acc, sel, perm, ystack, zbuf, tally, gath, stat, pstage, precv,
                dbsem, rowsem, gss, grs, sts, srs, pss, prs):
    ng = nd // 4
    keys = kt.shape[0]
    q = lax.axis_index("query")
    d = lax.axis_index("db")
    up = lax.rem(q + nq - 1, nq)
    down = lax.rem(q + 1, nq)
    lo_me = d // ng
    g_me = lax.rem(d, ng)

    def db_copy(i):
        return pltpu.make_async_copy(db_hbm.at[:, pl.ds(i * BLOCK, BLOCK)], dbv.at[i], dbsem.at[i])

    for i in range(dbv.shape[0]):
        db_copy(i).start()

    barrier = pltpu.get_barrier_semaphore()

    def greet(row, first):
        for o in range(first, nd):
            pl.semaphore_signal(barrier, inc=1, device_id=(row, lax.rem(d + o, nd)), device_id_type=MESH)

    for row in (up, down):
        pl.semaphore_signal(barrier, inc=1, device_id=(row, d), device_id_type=MESH)
    greet(q, 1)

    own_tile = noisy_ref[0].astype(BF16)
    gath[lo_me, g_me, 0] = own_tile

    def fill_sel(j, carry):
        lane = lax.broadcasted_iota(jnp.int32, (512, 128), 1)
        row = lax.broadcasted_iota(jnp.int32, (512, 128), 0)
        want = (lane // 32) * 128 + (4 * (lane % 32) + j) % 128
        sel[:, pl.ds(pl.multiple_of(j * 128, 128), 128)] = jnp.where(row == want, 1.0, 0.0).astype(BF16)
        return carry

    lax.fori_loop(0, 12, fill_sel, 0)

    def fill_perm(r, carry):
        row = lax.broadcasted_iota(jnp.int32, (144, 192), 0)
        col = lax.broadcasted_iota(jnp.int32, (144, 192), 1)
        want = (row % 12) * 16 + 4 * r + row // 12
        perm[pl.ds(pl.multiple_of(r * 144, 144), 144), :] = jnp.where(col == want, 1.0, 0.0).astype(BF16)
        return carry

    lax.fori_loop(0, 2, fill_perm, 0)

    pl.semaphore_wait(barrier, nd + 1)
    for row in (up, down):
        pl.semaphore_signal(rowsem, inc=1, device_id=(row, d), device_id_type=MESH)

    def tile_copy(half, o):
        return pltpu.make_async_remote_copy(
            src_ref=gath.at[lo_me, g_me, 0], dst_ref=gath.at[lo_me, g_me, half],
            send_sem=gss.at[half], recv_sem=grs.at[half],
            device_id=(up if half else q, lax.rem(d + o, nd)), device_id_type=MESH)

    def take(region, sem):
        pltpu.make_async_copy(region, region, sem).wait()

    def tiles(half):
        return tally.at[pl.ds(0, nd - 1 + half)]

    def over_peers(step, first=1):
        for o in range(first, nd):
            step(o)

    over_peers(lambda o: tile_copy(0, o).start())
    pl.semaphore_wait(rowsem, 2)
    over_peers(lambda o: tile_copy(1, o).start(), 0)

    for i in range(dbv.shape[0]):
        db_copy(i).wait()

    def key_columns(i, size):
        slot = i // (BLOCK // size)
        inside = pl.multiple_of(lax.rem(i, BLOCK // size) * size, size)
        return dbv[picked_ref[0, slot], :, pl.ds(inside, size)]

    def prepare(i, carry):
        cols = key_columns(i, PREP)
        wide = cols.astype(F32)
        squares = jnp.sum(wide * wide, axis=0, keepdims=True)
        high = squares.astype(BF16).astype(F32)
        rest = squares - high
        mid = rest.astype(BF16).astype(F32)
        low = rest - mid
        row = lax.broadcasted_iota(jnp.int32, (80, PREP), 0)
        extra = jnp.where((row == 0) | (row == 3) | (row == 5), high,
                          jnp.where((row == 1) | (row == 4), mid, jnp.where(row == 2, low, 0.0)))
        full = jnp.concatenate([cols, extra.astype(BF16)], axis=0)
        kt[pl.ds(pl.multiple_of(i * PREP, PREP), PREP), :] = full.T
        return carry

    lax.fori_loop(0, keys // PREP, prepare, 0)

    def per_lane(ref, g, rows):
        lane = lax.broadcasted_iota(jnp.int32, (rows, 256), 1)
        image = (lane // 32) % 4
        value = jnp.full((rows, 256), ref[g], F32)
        for lo in range(1, 4):
            value = jnp.where(image == lo, ref[lo * ng + g], value)
        return value

    for g in range(ng):
        a = per_lane(now_ref, g, 80)
        c = -0.5 * jnp.sqrt(a)
        high = c.astype(BF16).astype(F32)
        rest = c - high
        mid = rest.astype(BF16).astype(F32)
        low = rest - mid
        row = lax.broadcasted_iota(jnp.int32, (80, 256), 0)
        extra = jnp.where(row < 3, high, jnp.where(row < 5, mid, jnp.where(row == 5, low, 0.0)))
        qbuf[g, pl.ds(432, 80), :] = extra.astype(BF16)

    for half in range(2):
        take(tiles(half), grs.at[half])

    lanes = []
    for lo in range(4):
        both = jnp.concatenate([gath[lo, :, 0].astype(F32), gath[lo, :, 1].astype(F32)], axis=2)
        lanes.append(both.reshape(ng * 48, 128))
    rows = jnp.concatenate(lanes, axis=1).astype(BF16)
    for pair in range(6):
        y = jnp.dot(rows, sel[:, pair * 256:(pair + 1) * 256], preferred_element_type=F32).astype(BF16)
        for g in range(ng):
            for c in range(3):
                for k in range(2):
                    j = 2 * pair + k
                    ystack[c, j * 16:(j + 1) * 16, g * 128:(g + 1) * 128] = (
                        y[(g * 3 + c) * 16:(g * 3 + c + 1) * 16, k * 128:(k + 1) * 128])
    for c in range(3):
        placed = jnp.dot(perm[...], ystack[c], preferred_element_type=F32).astype(BF16)
        for g in range(ng):
            for r in range(2):
                qbuf[g, c * 144:(c + 1) * 144, r * 128:(r + 1) * 128] = (
                    placed[r * 144:(r + 1) * 144, g * 128:(g + 1) * 128])

    sbufs = (sbuf0, sbuf1)
    wbufs = (wbuf0, wbuf1, wbuf2)
    steps = keys // STEP

    def logits(g, start, size):
        part = pl.ds(start, size)
        s = jnp.dot(kt[part, :], qbuf[g], preferred_element_type=F32)
        sbufs[g % 2][part, :] = s
        return jnp.max(s.reshape(size // 8, 8, 256), axis=0)

    def weigh(g, start, size, top, scale):
        total = jnp.zeros((8, 256), F32)
        for k in range(size // CHUNK):
            part = pl.ds(start + k * CHUNK, CHUNK)
            p = jnp.exp2((sbufs[g % 2][part, :] - top) * scale)
            wbufs[g % 3][part, :] = p.astype(BF16)
            total = total + jnp.sum(p.reshape(CHUNK // 8, 8, 256), axis=0)
        return total

    def gather_keys(g, slot, inside, start, size):
        cols = dbv[picked_ref[0, slot], :, inside:inside + size]
        acc[g] += jnp.dot(cols, wbufs[g % 3][pl.ds(start, size), :], preferred_element_type=F32)

    def scale_of(g):
        a = per_lane(now_ref, g, 1)
        return LOG2E * jnp.sqrt(a) / (1.0 - a)

    def stat_send(g, o):
        return pltpu.make_async_remote_copy(
            src_ref=stat.at[g, d], dst_ref=stat.at[g, d], send_sem=sts.at[g], recv_sem=srs.at[g],
            device_id=(q, lax.rem(d + o, nd)), device_id_type=MESH)

    def share(g, top, total):
        whole = jnp.concatenate([top[:, :128], top[:, 128:], total[:, :128], total[:, 128:],
                                 jnp.zeros((4, 128), F32)], axis=0)
        stat[g, d] = whole
        over_peers(lambda o: stat_send(g, o).start())

    def pixel_send(g, lo, half):
        dest = lo * ng + g
        return pltpu.make_async_remote_copy(
            src_ref=pstage.at[g, lo, half], dst_ref=precv.at[half, d],
            send_sem=pss.at[g, 2 * lo + half], recv_sem=prs.at[half],
            device_id=(down if half else q, dest), device_id_type=MESH)

    def finish(g, top, scale):
        take(stat.at[g, pl.ds(0, nd - 1)], srs.at[g])
        every = stat[g]
        tops = jnp.concatenate([every[:, 0], every[:, 1]], axis=1)
        totals = jnp.concatenate([every[:, 2], every[:, 3]], axis=1)
        highest = jnp.max(tops, axis=0, keepdims=True)
        total = jnp.sum(totals * jnp.exp2((tops - highest) * scale), axis=0, keepdims=True)
        factor = jnp.exp2((top - highest) * scale) / (9.0 * total)
        num = acc[g] * factor
        for c in range(3):
            first = num[c * 144:(c + 1) * 144, :128]
            second = num[c * 144:(c + 1) * 144, 128:]
            zbuf[c * 192:c * 192 + 48, :] = first[:48]
            zbuf[c * 192 + 48:c * 192 + 144, :] = first[48:] + second[:96]
            zbuf[c * 192 + 144:c * 192 + 192, :] = second[96:]
        place = lax.broadcasted_iota(jnp.int32, (48, 128), 1) % 32
        parts = []
        for j in range(4):
            piece = zbuf[pl.ds(j, 48, stride=12), :]
            for k in (1, 2):
                z = zbuf[pl.ds(4 * k + j, 48, stride=12), :]
                piece = piece + jnp.where(place >= k, pltpu.roll(z, k, 1), pltpu.roll(z, 96 + k, 1))
            parts.append(piece)
        flat = jnp.concatenate(parts, axis=1)
        high = flat.astype(BF16)
        low = (flat - high.astype(F32)).astype(BF16)
        both = jnp.concatenate([high, low], axis=0)
        pix = lax.dot_general(both, sel[:, :512], (((1,), (1,)), ((), ())), preferred_element_type=F32)
        pix = pix[:48] + pix[48:]
        for lo in range(4):
            tile = pix[:, lo * 128:(lo + 1) * 128].reshape(3, 16, 128)
            pstage[g, lo, 0] = tile[:, :8]
            pstage[g, lo, 1] = tile[:, 8:]
        for lo in range(4):
            @pl.when(lo * ng + g != d)
            def _():
                pixel_send(g, lo, 0).start()
            pixel_send(g, lo, 1).start()

    neg = jnp.full((8, 256), -jnp.inf, F32)
    tops = {}
    scales = {}
    def phase(first=None, second=None, third=None):
        size = SUB // 2 if second is not None and (first is None or third is None) else SUB

        if second is not None:
            scales[second] = scale_of(second)
        if third is not None:
            acc[third] = jnp.zeros((432, 256), F32)

        def body(i, carry):
            best, total = carry
            base = pl.multiple_of(i * STEP, STEP)
            for b in range(STEP // size):
                start = base + b * size
                if first is not None:
                    best = jnp.maximum(best, logits(first, start, size))
                if second is not None:
                    total = total + weigh(second, start, size, tops[second], scales[second])
                if third is not None:
                    gather_keys(third, i, b * size, start, size)
            return best, total

        best, total = lax.fori_loop(0, steps, body, (neg, jnp.zeros((8, 256), F32)))
        if first is not None:
            tops[first] = jnp.max(best, axis=0, keepdims=True)
        if second is not None:
            share(second, tops[second], jnp.sum(total, axis=0, keepdims=True))
        if third is not None:
            finish(third, tops[third], scales[third])

    last = ng - 1
    for t in range(ng):
        phase(t, t - 1 if t >= 1 else None, t - 2 if 2 <= t < last else None)
    phase(None, last, max(last - 2, 0))
    for t in range(max(last - 2, 0) + 1, ng):
        phase(None, None, t)

    for half in range(2):
        take(tiles(half), gss.at[half])
    for g in range(ng):
        take(stat.at[g, pl.ds(0, nd - 1)], sts.at[g])
        for lo in range(4):
            @pl.when(lo * ng + g != d)
            def _():
                pixel_send(g, lo, 0).wait_send()
            pixel_send(g, lo, 1).wait_send()
    take(precv.at[0, pl.ds(0, nd - 1)], prs.at[0])
    take(precv.at[1], prs.at[1])
    precv[0, d] = pstage[g_me, lo_me, 0]
    denoised = jnp.sum(precv[0], axis=0) + jnp.sum(precv[1], axis=0)
    signal = jnp.full((1, 8, 128), now_ref[d], F32)
    after = jnp.full((1, 8, 128), next_ref[d], F32)
    noise = (noisy_ref[0] - jnp.sqrt(signal) * denoised) / jnp.sqrt(1.0 - signal)
    out_ref[0] = jnp.sqrt(after) * denoised + jnp.sqrt(1.0 - after) * noise


def on_device(nq, nd, noisy, database, picked, now, after):
    ng = nd // 4
    windows = picked.shape[1]
    keys = windows * BLOCK
    vmem = pl.BlockSpec(memory_space=pltpu.VMEM)
    smem = pl.BlockSpec(memory_space=pltpu.SMEM)
    dma = pltpu.SemaphoreType.DMA
    return pl.pallas_call(
        functools.partial(step_kernel, nq, nd),
        out_shape=jax.ShapeDtypeStruct(noisy.shape, F32),
        in_specs=[vmem, pl.BlockSpec(memory_space=pl.ANY), smem, smem, smem],
        out_specs=vmem,
        scratch_shapes=[
            pltpu.VMEM((database.shape[1] // BLOCK, database.shape[0], BLOCK), BF16),
            pltpu.VMEM((keys, 512), BF16),
            pltpu.VMEM((keys, 256), F32),
            pltpu.VMEM((keys, 256), F32),
            pltpu.VMEM((keys, 256), BF16),
            pltpu.VMEM((keys, 256), BF16),
            pltpu.VMEM((keys, 256), BF16),
            pltpu.VMEM((ng, 512, 256), BF16),
            pltpu.VMEM((ng, 432, 256), F32),
            pltpu.VMEM((512, 1536), BF16),
            pltpu.VMEM((288, 192), BF16),
            pltpu.VMEM((3, 192, ng * 128), BF16),
            pltpu.VMEM((576, 128), F32),
            pltpu.VMEM((nd, 3, 8, 128), BF16),
            pltpu.VMEM((4, ng, 2, 3, 8, 128), BF16),
            pltpu.VMEM((ng, nd, 8, 128), F32),
            pltpu.VMEM((ng, 4, 2, 3, 8, 128), F32),
            pltpu.VMEM((2, nd, 3, 8, 128), F32),
            dma((database.shape[1] // BLOCK,)),
            pltpu.SemaphoreType.REGULAR,
            dma((2,)),
            dma((2,)),
            dma((ng,)),
            dma((ng,)),
            dma((ng, 8)),
            dma((2,)),
        ],
        compiler_params=pltpu.CompilerParams(
            collective_id=0, has_side_effects=True, vmem_limit_bytes=64_000_000),
    )(noisy, database, picked, now, after)


def solution(mesh):
    return jax.shard_map(
        functools.partial(on_device, mesh.shape["query"], mesh.shape["db"]),
        mesh=mesh,
        in_specs=(P("db", None, "query", None), P(None, "db"), P("db", None), P(), P()),
        out_specs=P("db", None, "query", None),
        check_vma=False,
    )
```

```python
import functools

import jax
import jax.numpy as jnp
from jax import lax
from jax.experimental import pallas as pl
from jax.experimental.pallas import tpu as pltpu
from jax.sharding import PartitionSpec as P

MESH = pl.DeviceIdType.MESH
F32 = jnp.float32
BF16 = jnp.bfloat16
BLOCK = 2048
PREP = 512
STEP = 2048
SUB = 512
CHUNK = 32
LOG2E = 1.4426950408889634


def step_kernel(nq, nd, noisy_ref, db_hbm, picked_ref, now_ref, next_ref, out_ref,
                dbv, kt, sbuf0, sbuf1, wbuf0, wbuf1, wbuf2, qbuf, acc, sel, perm, ystack, zbuf, tally, gath, stat, pstage, precv,
                dbsem, gss, grs, sts, srs, pss, prs):
    ng = nd // 4
    keys = kt.shape[0]
    q = lax.axis_index("query")
    d = lax.axis_index("db")
    up = lax.rem(q + nq - 1, nq)
    down = lax.rem(q + 1, nq)
    lo_me = d // ng
    g_me = lax.rem(d, ng)

    def db_copy(i):
        return pltpu.make_async_copy(db_hbm.at[:, pl.ds(i * BLOCK, BLOCK)], dbv.at[i], dbsem.at[i])

    for i in range(dbv.shape[0]):
        db_copy(i).start()

    barrier = pltpu.get_barrier_semaphore()

    def greet(row, first):
        for o in range(first, nd):
            pl.semaphore_signal(barrier, inc=1, device_id=(row, lax.rem(d + o, nd)), device_id_type=MESH)

    for row in (up, down):
        pl.semaphore_signal(barrier, inc=1, device_id=(row, d), device_id_type=MESH)
    greet(q, 1)

    own_tile = noisy_ref[0].astype(BF16)
    gath[lo_me, g_me, 0] = own_tile

    pl.semaphore_wait(barrier, nd + 1)

    def column_copy():
        return pltpu.make_async_remote_copy(
            src_ref=gath.at[lo_me, g_me, 0], dst_ref=gath.at[lo_me, g_me, 1],
            send_sem=gss.at[0], recv_sem=grs.at[0], device_id=(up, d), device_id_type=MESH)

    def row_copy(half, o):
        return pltpu.make_async_remote_copy(
            src_ref=gath.at[lo_me, g_me, half], dst_ref=gath.at[lo_me, g_me, half],
            send_sem=gss.at[1 + half], recv_sem=grs.at[1 + half],
            device_id=(q, lax.rem(d + o, nd)), device_id_type=MESH)

    def take(region, sem):
        pltpu.make_async_copy(region, region, sem).wait()

    def over_peers(step, first=1):
        for o in range(first, nd):
            step(o)

    column_copy().start()
    over_peers(lambda o: row_copy(0, o).start())

    def fill_sel(j, carry):
        lane = lax.broadcasted_iota(jnp.int32, (512, 128), 1)
        row = lax.broadcasted_iota(jnp.int32, (512, 128), 0)
        want = (lane // 32) * 128 + (4 * (lane % 32) + j) % 128
        sel[:, pl.ds(pl.multiple_of(j * 128, 128), 128)] = jnp.where(row == want, 1.0, 0.0).astype(BF16)
        return carry

    lax.fori_loop(0, 12, fill_sel, 0)

    def fill_perm(r, carry):
        row = lax.broadcasted_iota(jnp.int32, (144, 192), 0)
        col = lax.broadcasted_iota(jnp.int32, (144, 192), 1)
        want = (row % 12) * 16 + 4 * r + row // 12
        perm[pl.ds(pl.multiple_of(r * 144, 144), 144), :] = jnp.where(col == want, 1.0, 0.0).astype(BF16)
        return carry

    lax.fori_loop(0, 2, fill_perm, 0)

    column_copy().wait_recv()
    over_peers(lambda o: row_copy(1, o).start())

    for i in range(dbv.shape[0]):
        db_copy(i).wait()

    def key_columns(i, size):
        slot = i // (BLOCK // size)
        inside = pl.multiple_of(lax.rem(i, BLOCK // size) * size, size)
        return dbv[picked_ref[0, slot], :, pl.ds(inside, size)]

    def prepare(i, carry):
        cols = key_columns(i, PREP)
        wide = cols.astype(F32)
        squares = jnp.sum(wide * wide, axis=0, keepdims=True)
        high = squares.astype(BF16).astype(F32)
        rest = squares - high
        mid = rest.astype(BF16).astype(F32)
        low = rest - mid
        row = lax.broadcasted_iota(jnp.int32, (80, PREP), 0)
        extra = jnp.where((row == 0) | (row == 3) | (row == 5), high,
                          jnp.where((row == 1) | (row == 4), mid, jnp.where(row == 2, low, 0.0)))
        full = jnp.concatenate([cols, extra.astype(BF16)], axis=0)
        kt[pl.ds(pl.multiple_of(i * PREP, PREP), PREP), :] = full.T
        return carry

    lax.fori_loop(0, keys // PREP, prepare, 0)

    def per_lane(ref, g, rows):
        lane = lax.broadcasted_iota(jnp.int32, (rows, 256), 1)
        image = (lane // 32) % 4
        value = jnp.full((rows, 256), ref[g], F32)
        for lo in range(1, 4):
            value = jnp.where(image == lo, ref[lo * ng + g], value)
        return value

    for g in range(ng):
        a = per_lane(now_ref, g, 80)
        c = -0.5 * jnp.sqrt(a)
        high = c.astype(BF16).astype(F32)
        rest = c - high
        mid = rest.astype(BF16).astype(F32)
        low = rest - mid
        row = lax.broadcasted_iota(jnp.int32, (80, 256), 0)
        extra = jnp.where(row < 3, high, jnp.where(row < 5, mid, jnp.where(row == 5, low, 0.0)))
        qbuf[g, pl.ds(432, 80), :] = extra.astype(BF16)

    for half in range(2):
        take(tally, grs.at[1 + half])

    lanes = []
    for lo in range(4):
        both = jnp.concatenate([gath[lo, :, 0].astype(F32), gath[lo, :, 1].astype(F32)], axis=2)
        lanes.append(both.reshape(ng * 48, 128))
    rows = jnp.concatenate(lanes, axis=1).astype(BF16)
    for pair in range(6):
        y = jnp.dot(rows, sel[:, pair * 256:(pair + 1) * 256], preferred_element_type=F32).astype(BF16)
        for g in range(ng):
            for c in range(3):
                for k in range(2):
                    j = 2 * pair + k
                    ystack[c, j * 16:(j + 1) * 16, g * 128:(g + 1) * 128] = (
                        y[(g * 3 + c) * 16:(g * 3 + c + 1) * 16, k * 128:(k + 1) * 128])
    for c in range(3):
        placed = jnp.dot(perm[...], ystack[c], preferred_element_type=F32).astype(BF16)
        for g in range(ng):
            for r in range(2):
                qbuf[g, c * 144:(c + 1) * 144, r * 128:(r + 1) * 128] = (
                    placed[r * 144:(r + 1) * 144, g * 128:(g + 1) * 128])

    sbufs = (sbuf0, sbuf1)
    wbufs = (wbuf0, wbuf1, wbuf2)
    steps = keys // STEP

    def logits(g, start, size):
        part = pl.ds(start, size)
        s = jnp.dot(kt[part, :], qbuf[g], preferred_element_type=F32)
        sbufs[g % 2][part, :] = s
        return jnp.max(s.reshape(size // 8, 8, 256), axis=0)

    def weigh(g, start, size, top, scale):
        total = jnp.zeros((8, 256), F32)
        for k in range(size // CHUNK):
            part = pl.ds(start + k * CHUNK, CHUNK)
            p = jnp.exp2((sbufs[g % 2][part, :] - top) * scale)
            wbufs[g % 3][part, :] = p.astype(BF16)
            total = total + jnp.sum(p.reshape(CHUNK // 8, 8, 256), axis=0)
        return total

    def gather_keys(g, slot, inside, start, size):
        cols = dbv[picked_ref[0, slot], :, inside:inside + size]
        acc[g] += jnp.dot(cols, wbufs[g % 3][pl.ds(start, size), :], preferred_element_type=F32)

    def scale_of(g):
        a = per_lane(now_ref, g, 1)
        return LOG2E * jnp.sqrt(a) / (1.0 - a)

    def stat_send(g, o):
        return pltpu.make_async_remote_copy(
            src_ref=stat.at[g, d], dst_ref=stat.at[g, d], send_sem=sts.at[g], recv_sem=srs.at[g],
            device_id=(q, lax.rem(d + o, nd)), device_id_type=MESH)

    def share(g, top, total):
        whole = jnp.concatenate([top[:, :128], top[:, 128:], total[:, :128], total[:, 128:],
                                 jnp.zeros((4, 128), F32)], axis=0)
        stat[g, d] = whole
        over_peers(lambda o: stat_send(g, o).start())

    def pixel_send(g, lo, half):
        dest = lo * ng + g
        return pltpu.make_async_remote_copy(
            src_ref=pstage.at[g, lo, half], dst_ref=precv.at[half, d],
            send_sem=pss.at[g, 2 * lo + half], recv_sem=prs.at[half],
            device_id=(down if half else q, dest), device_id_type=MESH)

    def finish(g, top, scale):
        take(stat.at[g, pl.ds(0, nd - 1)], srs.at[g])
        every = stat[g]
        tops = jnp.concatenate([every[:, 0], every[:, 1]], axis=1)
        totals = jnp.concatenate([every[:, 2], every[:, 3]], axis=1)
        highest = jnp.max(tops, axis=0, keepdims=True)
        total = jnp.sum(totals * jnp.exp2((tops - highest) * scale), axis=0, keepdims=True)
        factor = jnp.exp2((top - highest) * scale) / (9.0 * total)
        num = acc[g] * factor
        for c in range(3):
            first = num[c * 144:(c + 1) * 144, :128]
            second = num[c * 144:(c + 1) * 144, 128:]
            zbuf[c * 192:c * 192 + 48, :] = first[:48]
            zbuf[c * 192 + 48:c * 192 + 144, :] = first[48:] + second[:96]
            zbuf[c * 192 + 144:c * 192 + 192, :] = second[96:]
        place = lax.broadcasted_iota(jnp.int32, (48, 128), 1) % 32
        parts = []
        for j in range(4):
            piece = zbuf[pl.ds(j, 48, stride=12), :]
            for k in (1, 2):
                z = zbuf[pl.ds(4 * k + j, 48, stride=12), :]
                piece = piece + jnp.where(place >= k, pltpu.roll(z, k, 1), pltpu.roll(z, 96 + k, 1))
            parts.append(piece)
        flat = jnp.concatenate(parts, axis=1)
        high = flat.astype(BF16)
        low = (flat - high.astype(F32)).astype(BF16)
        both = jnp.concatenate([high, low], axis=0)
        pix = lax.dot_general(both, sel[:, :512], (((1,), (1,)), ((), ())), preferred_element_type=F32)
        pix = pix[:48] + pix[48:]
        for lo in range(4):
            tile = pix[:, lo * 128:(lo + 1) * 128].reshape(3, 16, 128)
            pstage[g, lo, 0] = tile[:, :8]
            pstage[g, lo, 1] = tile[:, 8:]
        for lo in range(4):
            pixel_send(g, lo, 1).start()
        for lo in range(4):
            @pl.when(lo * ng + g != d)
            def _():
                pixel_send(g, lo, 0).start()

    neg = jnp.full((8, 256), -jnp.inf, F32)
    tops = {}
    scales = {}
    def phase(first=None, second=None, third=None):
        size = SUB // 2 if second is not None and (first is None or third is None) else SUB

        if second is not None:
            scales[second] = scale_of(second)
        if third is not None:
            acc[third] = jnp.zeros((432, 256), F32)

        def body(i, carry):
            best, total = carry
            base = pl.multiple_of(i * STEP, STEP)
            for b in range(STEP // size):
                start = base + b * size
                if first is not None:
                    best = jnp.maximum(best, logits(first, start, size))
                if second is not None:
                    total = total + weigh(second, start, size, tops[second], scales[second])
                if third is not None:
                    gather_keys(third, i, b * size, start, size)
            return best, total

        best, total = lax.fori_loop(0, steps, body, (neg, jnp.zeros((8, 256), F32)))
        if first is not None:
            tops[first] = jnp.max(best, axis=0, keepdims=True)
        if second is not None:
            share(second, tops[second], jnp.sum(total, axis=0, keepdims=True))
        if third is not None:
            finish(third, tops[third], scales[third])

    last = ng - 1
    for t in range(ng):
        phase(t, t - 1 if t >= 1 else None, t - 2 if 2 <= t < last else None)
    phase(None, last, max(last - 2, 0))
    for t in range(max(last - 2, 0) + 1, ng):
        phase(None, None, t)

    column_copy().wait_send()
    for half in range(2):
        take(tally, gss.at[1 + half])
    for g in range(ng):
        take(stat.at[g, pl.ds(0, nd - 1)], sts.at[g])
        for lo in range(4):
            @pl.when(lo * ng + g != d)
            def _():
                pixel_send(g, lo, 0).wait_send()
            pixel_send(g, lo, 1).wait_send()
    take(precv.at[0, pl.ds(0, nd - 1)], prs.at[0])
    take(precv.at[1], prs.at[1])
    precv[0, d] = pstage[g_me, lo_me, 0]
    denoised = jnp.sum(precv[0], axis=0) + jnp.sum(precv[1], axis=0)
    signal = jnp.full((1, 8, 128), now_ref[d], F32)
    after = jnp.full((1, 8, 128), next_ref[d], F32)
    noise = (noisy_ref[0] - jnp.sqrt(signal) * denoised) / jnp.sqrt(1.0 - signal)
    out_ref[0] = jnp.sqrt(after) * denoised + jnp.sqrt(1.0 - after) * noise


def on_device(nq, nd, noisy, database, picked, now, after):
    ng = nd // 4
    windows = picked.shape[1]
    keys = windows * BLOCK
    vmem = pl.BlockSpec(memory_space=pltpu.VMEM)
    smem = pl.BlockSpec(memory_space=pltpu.SMEM)
    dma = pltpu.SemaphoreType.DMA
    return pl.pallas_call(
        functools.partial(step_kernel, nq, nd),
        out_shape=jax.ShapeDtypeStruct(noisy.shape, F32),
        in_specs=[vmem, pl.BlockSpec(memory_space=pl.ANY), smem, smem, smem],
        out_specs=vmem,
        scratch_shapes=[
            pltpu.VMEM((database.shape[1] // BLOCK, database.shape[0], BLOCK), BF16),
            pltpu.VMEM((keys, 512), BF16),
            pltpu.VMEM((keys, 256), F32),
            pltpu.VMEM((keys, 256), F32),
            pltpu.VMEM((keys, 256), BF16),
            pltpu.VMEM((keys, 256), BF16),
            pltpu.VMEM((keys, 256), BF16),
            pltpu.VMEM((ng, 512, 256), BF16),
            pltpu.VMEM((ng, 432, 256), F32),
            pltpu.VMEM((512, 1536), BF16),
            pltpu.VMEM((288, 192), BF16),
            pltpu.VMEM((3, 192, ng * 128), BF16),
            pltpu.VMEM((576, 128), F32),
            pltpu.VMEM((nd - 1, 3, 8, 128), BF16),
            pltpu.VMEM((4, ng, 2, 3, 8, 128), BF16),
            pltpu.VMEM((ng, nd, 8, 128), F32),
            pltpu.VMEM((ng, 4, 2, 3, 8, 128), F32),
            pltpu.VMEM((2, nd, 3, 8, 128), F32),
            dma((database.shape[1] // BLOCK,)),
            dma((3,)),
            dma((3,)),
            dma((ng,)),
            dma((ng,)),
            dma((ng, 8)),
            dma((2,)),
        ],
        compiler_params=pltpu.CompilerParams(
            collective_id=0, has_side_effects=True, vmem_limit_bytes=64_000_000),
    )(noisy, database, picked, now, after)


def solution(mesh):
    return jax.shard_map(
        functools.partial(on_device, mesh.shape["query"], mesh.shape["db"]),
        mesh=mesh,
        in_specs=(P("db", None, "query", None), P(None, "db"), P("db", None), P(), P()),
        out_specs=P("db", None, "query", None),
        check_vma=False,
    )
```

```python
import functools

import jax
import jax.numpy as jnp
from jax import lax
from jax.experimental import pallas as pl
from jax.experimental.pallas import tpu as pltpu
from jax.sharding import PartitionSpec as P

MESH = pl.DeviceIdType.MESH
F32 = jnp.float32
BF16 = jnp.bfloat16
BLOCK = 2048
PREP = 512
STEP = 2048
SUB = 512
CHUNK = 32
LOG2E = 1.4426950408889634


def step_kernel(nq, nd, noisy_ref, db_hbm, picked_ref, now_ref, next_ref, out_ref,
                dbv, kt, sbuf0, sbuf1, wbuf0, wbuf1, wbuf2, qbuf, acc, sel, perm, ystack, zbuf, tally, gath, stat, pstage, precv,
                dbsem, gss, grs, sts, srs, pss, prs):
    ng = nd // 4
    keys = kt.shape[0]
    q = lax.axis_index("query")
    d = lax.axis_index("db")
    up = lax.rem(q + nq - 1, nq)
    down = lax.rem(q + 1, nq)
    lo_me = d // ng
    g_me = lax.rem(d, ng)

    def db_copy(i):
        return pltpu.make_async_copy(db_hbm.at[:, pl.ds(i * BLOCK, BLOCK)], dbv.at[i], dbsem.at[i])

    for i in range(dbv.shape[0]):
        db_copy(i).start()

    barrier = pltpu.get_barrier_semaphore()

    def greet(row, first):
        for o in range(first, nd):
            pl.semaphore_signal(barrier, inc=1, device_id=(row, lax.rem(d + o, nd)), device_id_type=MESH)

    for row in (up, down):
        pl.semaphore_signal(barrier, inc=1, device_id=(row, d), device_id_type=MESH)
    greet(q, 1)

    own_tile = noisy_ref[0].astype(BF16)
    gath[lo_me, g_me, 0] = own_tile

    pl.semaphore_wait(barrier, nd + 1)

    def column_copy():
        return pltpu.make_async_remote_copy(
            src_ref=gath.at[lo_me, g_me, 0], dst_ref=gath.at[lo_me, g_me, 1],
            send_sem=gss.at[0], recv_sem=grs.at[0], device_id=(up, d), device_id_type=MESH)

    def row_copy(half, o):
        return pltpu.make_async_remote_copy(
            src_ref=gath.at[lo_me, g_me, half], dst_ref=gath.at[lo_me, g_me, half],
            send_sem=gss.at[1 + half], recv_sem=grs.at[1 + half],
            device_id=(q, lax.rem(d + o, nd)), device_id_type=MESH)

    def take(region, sem):
        pltpu.make_async_copy(region, region, sem).wait()

    def over_peers(step, first=1):
        for o in range(first, nd):
            step(o)

    column_copy().start()
    over_peers(lambda o: row_copy(0, o).start())

    def fill_sel(j, carry):
        lane = lax.broadcasted_iota(jnp.int32, (512, 128), 1)
        row = lax.broadcasted_iota(jnp.int32, (512, 128), 0)
        want = (lane // 32) * 128 + (4 * (lane % 32) + j) % 128
        sel[:, pl.ds(pl.multiple_of(j * 128, 128), 128)] = jnp.where(row == want, 1.0, 0.0).astype(BF16)
        return carry

    lax.fori_loop(0, 4, fill_sel, 0)

    def fill_perm(r, carry):
        row = lax.broadcasted_iota(jnp.int32, (144, 192), 0)
        col = lax.broadcasted_iota(jnp.int32, (144, 192), 1)
        want = (row % 12) * 16 + 4 * r + row // 12
        perm[pl.ds(pl.multiple_of(r * 144, 144), 144), :] = jnp.where(col == want, 1.0, 0.0).astype(BF16)
        return carry

    lax.fori_loop(0, 2, fill_perm, 0)

    column_copy().wait_recv()
    over_peers(lambda o: row_copy(1, o).start())

    for i in range(dbv.shape[0]):
        db_copy(i).wait()

    def key_columns(i, size):
        slot = i // (BLOCK // size)
        inside = pl.multiple_of(lax.rem(i, BLOCK // size) * size, size)
        return dbv[picked_ref[0, slot], :, pl.ds(inside, size)]

    def prepare(i, carry):
        cols = key_columns(i, PREP)
        wide = cols.astype(F32)
        squares = jnp.sum(wide * wide, axis=0, keepdims=True)
        high = squares.astype(BF16).astype(F32)
        rest = squares - high
        mid = rest.astype(BF16).astype(F32)
        low = rest - mid
        row = lax.broadcasted_iota(jnp.int32, (80, PREP), 0)
        extra = jnp.where((row == 0) | (row == 3) | (row == 5), high,
                          jnp.where((row == 1) | (row == 4), mid, jnp.where(row == 2, low, 0.0)))
        full = jnp.concatenate([cols, extra.astype(BF16)], axis=0)
        kt[pl.ds(pl.multiple_of(i * PREP, PREP), PREP), :] = full.T
        return carry

    lax.fori_loop(0, keys // PREP, prepare, 0)

    def per_lane(ref, g, rows):
        lane = lax.broadcasted_iota(jnp.int32, (rows, 256), 1)
        image = (lane // 32) % 4
        value = jnp.full((rows, 256), ref[g], F32)
        for lo in range(1, 4):
            value = jnp.where(image == lo, ref[lo * ng + g], value)
        return value

    for g in range(ng):
        a = per_lane(now_ref, g, 80)
        c = -0.5 * jnp.sqrt(a)
        high = c.astype(BF16).astype(F32)
        rest = c - high
        mid = rest.astype(BF16).astype(F32)
        low = rest - mid
        row = lax.broadcasted_iota(jnp.int32, (80, 256), 0)
        extra = jnp.where(row < 3, high, jnp.where(row < 5, mid, jnp.where(row == 5, low, 0.0)))
        qbuf[g, pl.ds(432, 80), :] = extra.astype(BF16)

    def scale_of(g):
        a = per_lane(now_ref, g, 1)
        return LOG2E * jnp.sqrt(a) / (1.0 - a)

    scales = [scale_of(g) for g in range(ng)]
    acc[...] = jnp.zeros(acc.shape, F32)

    for half in range(2):
        take(tally, grs.at[1 + half])

    lanes = []
    for lo in range(4):
        both = jnp.concatenate([gath[lo, :, 0].astype(F32), gath[lo, :, 1].astype(F32)], axis=2)
        lanes.append(both.reshape(ng * 48, 128))
    rows = jnp.concatenate(lanes, axis=1).astype(BF16)
    spread = jnp.dot(rows, sel[...], preferred_element_type=F32)
    place = lax.broadcasted_iota(jnp.int32, (ng * 48, 128), 1) % 32
    for k in range(4):
        first_columns = spread[:, k * 128:(k + 1) * 128]
        for shift in range(3):
            y = first_columns
            if shift:
                y = jnp.where(place < 32 - shift, pltpu.roll(y, 128 - shift, 1), pltpu.roll(y, 32 - shift, 1))
            y = y.astype(BF16)
            j = 4 * shift + k
            for g in range(ng):
                for c in range(3):
                    ystack[c, j * 16:(j + 1) * 16, g * 128:(g + 1) * 128] = y[(g * 3 + c) * 16:(g * 3 + c + 1) * 16, :]
    for c in range(3):
        placed = jnp.dot(perm[...], ystack[c], preferred_element_type=F32).astype(BF16)
        for g in range(ng):
            for r in range(2):
                qbuf[g, c * 144:(c + 1) * 144, r * 128:(r + 1) * 128] = (
                    placed[r * 144:(r + 1) * 144, g * 128:(g + 1) * 128])

    sbufs = (sbuf0, sbuf1)
    wbufs = (wbuf0, wbuf1, wbuf2)
    steps = keys // STEP

    def logits(g, start, size):
        part = pl.ds(start, size)
        s = jnp.dot(kt[part, :], qbuf[g], preferred_element_type=F32)
        sbufs[g % 2][part, :] = s
        return jnp.max(s.reshape(size // 8, 8, 256), axis=0)

    def weigh(g, start, size, top, scale):
        total = jnp.zeros((8, 256), F32)
        for k in range(size // CHUNK):
            part = pl.ds(start + k * CHUNK, CHUNK)
            p = jnp.exp2((sbufs[g % 2][part, :] - top) * scale)
            wbufs[g % 3][part, :] = p.astype(BF16)
            total = total + jnp.sum(p.reshape(CHUNK // 8, 8, 256), axis=0)
        return total

    def gather_keys(g, slot, inside, start, size):
        cols = dbv[picked_ref[0, slot], :, inside:inside + size]
        acc[g] += jnp.dot(cols, wbufs[g % 3][pl.ds(start, size), :], preferred_element_type=F32)

    def stat_send(g, o):
        return pltpu.make_async_remote_copy(
            src_ref=stat.at[g, d], dst_ref=stat.at[g, d], send_sem=sts.at[g], recv_sem=srs.at[g],
            device_id=(q, lax.rem(d + o, nd)), device_id_type=MESH)

    def share(g, top, total):
        whole = jnp.concatenate([top[:, :128], top[:, 128:], total[:, :128], total[:, 128:],
                                 jnp.zeros((4, 128), F32)], axis=0)
        stat[g, d] = whole
        over_peers(lambda o: stat_send(g, o).start())

    def pixel_send(g, lo, half):
        dest = lo * ng + g
        return pltpu.make_async_remote_copy(
            src_ref=pstage.at[g, lo, half], dst_ref=precv.at[half, d],
            send_sem=pss.at[g, 2 * lo + half], recv_sem=prs.at[half],
            device_id=(down if half else q, dest), device_id_type=MESH)

    def finish(g, top, scale):
        take(stat.at[g, pl.ds(0, nd - 1)], srs.at[g])
        every = stat[g]
        tops = jnp.concatenate([every[:, 0], every[:, 1]], axis=1)
        totals = jnp.concatenate([every[:, 2], every[:, 3]], axis=1)
        highest = jnp.max(tops, axis=0, keepdims=True)
        total = jnp.sum(totals * jnp.exp2((tops - highest) * scale), axis=0, keepdims=True)
        factor = jnp.exp2((top - highest) * scale) / (9.0 * total)
        num = acc[g] * factor
        for c in range(3):
            first = num[c * 144:(c + 1) * 144, :128]
            second = num[c * 144:(c + 1) * 144, 128:]
            zbuf[c * 192:c * 192 + 48, :] = first[:48]
            zbuf[c * 192 + 48:c * 192 + 144, :] = first[48:] + second[:96]
            zbuf[c * 192 + 144:c * 192 + 192, :] = second[96:]
        place = lax.broadcasted_iota(jnp.int32, (48, 128), 1) % 32
        parts = []
        for j in range(4):
            piece = zbuf[pl.ds(j, 48, stride=12), :]
            for k in (1, 2):
                z = zbuf[pl.ds(4 * k + j, 48, stride=12), :]
                piece = piece + jnp.where(place >= k, pltpu.roll(z, k, 1), pltpu.roll(z, 96 + k, 1))
            parts.append(piece)
        flat = jnp.concatenate(parts, axis=1)
        high = flat.astype(BF16)
        low = (flat - high.astype(F32)).astype(BF16)
        both = jnp.concatenate([high, low], axis=0)
        pix = lax.dot_general(both, sel[...], (((1,), (1,)), ((), ())), preferred_element_type=F32)
        pix = pix[:48] + pix[48:]
        for lo in range(4):
            tile = pix[:, lo * 128:(lo + 1) * 128].reshape(3, 16, 128)
            pstage[g, lo, 0] = tile[:, :8]
            pstage[g, lo, 1] = tile[:, 8:]
        for lo in range(4):
            pixel_send(g, lo, 1).start()
        for lo in range(4):
            @pl.when(lo * ng + g != d)
            def _():
                pixel_send(g, lo, 0).start()

    neg = jnp.full((8, 256), -jnp.inf, F32)
    tops = {}
    def phase(first=None, second=None, third=None):
        if second is not None and (first is None or third is None):
            size = SUB // 2
        else:
            size = SUB if third is not None else 2 * SUB

        def body(i, carry):
            best, total = carry
            base = pl.multiple_of(i * STEP, STEP)
            for b in range(STEP // size):
                start = base + b * size
                if first is not None:
                    best = jnp.maximum(best, logits(first, start, size))
                if second is not None:
                    total = total + weigh(second, start, size, tops[second], scales[second])
                if third is not None:
                    gather_keys(third, i, b * size, start, size)
            return best, total

        best, total = lax.fori_loop(0, steps, body, (neg, jnp.zeros((8, 256), F32)))
        if first is not None:
            tops[first] = jnp.max(best, axis=0, keepdims=True)
        if second is not None:
            share(second, tops[second], jnp.sum(total, axis=0, keepdims=True))
        if third is not None:
            finish(third, tops[third], scales[third])

    last = ng - 1
    for t in range(ng):
        phase(t, t - 1 if t >= 1 else None, t - 2 if 2 <= t < last else None)
    phase(None, last, max(last - 2, 0))
    for t in range(max(last - 2, 0) + 1, ng):
        phase(None, None, t)

    column_copy().wait_send()
    for half in range(2):
        take(tally, gss.at[1 + half])
    for g in range(ng):
        take(stat.at[g, pl.ds(0, nd - 1)], sts.at[g])
        for lo in range(4):
            @pl.when(lo * ng + g != d)
            def _():
                pixel_send(g, lo, 0).wait_send()
            pixel_send(g, lo, 1).wait_send()
    take(precv.at[0, pl.ds(0, nd - 1)], prs.at[0])
    take(precv.at[1], prs.at[1])
    precv[0, d] = pstage[g_me, lo_me, 0]
    denoised = jnp.sum(precv[0], axis=0) + jnp.sum(precv[1], axis=0)
    signal = jnp.full((1, 8, 128), now_ref[d], F32)
    after = jnp.full((1, 8, 128), next_ref[d], F32)
    noise = (noisy_ref[0] - jnp.sqrt(signal) * denoised) / jnp.sqrt(1.0 - signal)
    out_ref[0] = jnp.sqrt(after) * denoised + jnp.sqrt(1.0 - after) * noise


def on_device(nq, nd, noisy, database, picked, now, after):
    ng = nd // 4
    windows = picked.shape[1]
    keys = windows * BLOCK
    vmem = pl.BlockSpec(memory_space=pltpu.VMEM)
    smem = pl.BlockSpec(memory_space=pltpu.SMEM)
    dma = pltpu.SemaphoreType.DMA
    return pl.pallas_call(
        functools.partial(step_kernel, nq, nd),
        out_shape=jax.ShapeDtypeStruct(noisy.shape, F32),
        in_specs=[vmem, pl.BlockSpec(memory_space=pl.ANY), smem, smem, smem],
        out_specs=vmem,
        scratch_shapes=[
            pltpu.VMEM((database.shape[1] // BLOCK, database.shape[0], BLOCK), BF16),
            pltpu.VMEM((keys, 512), BF16),
            pltpu.VMEM((keys, 256), F32),
            pltpu.VMEM((keys, 256), F32),
            pltpu.VMEM((keys, 256), BF16),
            pltpu.VMEM((keys, 256), BF16),
            pltpu.VMEM((keys, 256), BF16),
            pltpu.VMEM((ng, 512, 256), BF16),
            pltpu.VMEM((ng, 432, 256), F32),
            pltpu.VMEM((512, 512), BF16),
            pltpu.VMEM((288, 192), BF16),
            pltpu.VMEM((3, 192, ng * 128), BF16),
            pltpu.VMEM((576, 128), F32),
            pltpu.VMEM((nd - 1, 3, 8, 128), BF16),
            pltpu.VMEM((4, ng, 2, 3, 8, 128), BF16),
            pltpu.VMEM((ng, nd, 8, 128), F32),
            pltpu.VMEM((ng, 4, 2, 3, 8, 128), F32),
            pltpu.VMEM((2, nd, 3, 8, 128), F32),
            dma((database.shape[1] // BLOCK,)),
            dma((3,)),
            dma((3,)),
            dma((ng,)),
            dma((ng,)),
            dma((ng, 8)),
            dma((2,)),
        ],
        compiler_params=pltpu.CompilerParams(
            collective_id=0, has_side_effects=True, vmem_limit_bytes=64_000_000),
    )(noisy, database, picked, now, after)


def solution(mesh):
    return jax.shard_map(
        functools.partial(on_device, mesh.shape["query"], mesh.shape["db"]),
        mesh=mesh,
        in_specs=(P("db", None, "query", None), P(None, "db"), P("db", None), P(), P()),
        out_specs=P("db", None, "query", None),
        check_vma=False,
    )
```
